32 devices in a mesh: section: 2 (over x), view: 8 (over z, y), scene: 2 (over core).
Axes of the slice: x: 2, y: 2, z: 4, core: 2. Of those that a mesh axis runs over, the one named last changes fastest.
Arguments:
- tokens: bfloat16 [2, 512, 1024], P('scene', ('section', 'view')), may hold values from -6 to 6
- norm_gain: float32 [1024], replicated, may hold values from 0.1 to 1.9
- head_weight: bfloat16 [1024, 512], replicated, may hold values from -0.1875 to 0.1875
- tile_lists: int32 [2, 64, 128], P('scene', ('section', 'view')), may hold values from 0 to 32767, as said below
- tile_counts: int32 [2, 64], P('scene', ('section', 'view')), may hold values from 1 to 128, as said below
- cameras: float32 [2, 2, 8], P('scene'), may hold values from -3 to 3
- targets: bfloat16 [2, 64, 768], P('scene', ('section', 'view')), may hold values from 0 to 1
Outputs:
- image: bfloat16 [2, 64, 768], P('scene', ('section', 'view'))
- grad_head: float32 [1024, 512], replicated
- loss: float32 [], replicated
The draws below stay inside these ranges and needn't reach their ends.
Inputs may be any that keep to these rules, and one draw needn't show every extreme that they name: `tile_lists`: gaussian n of a scene has owner n // 2048. Among the 512 slots (live or not) of each aligned block of 4 tiles, at most 64 name Gaussians of one owner, and in every such block some owner is named exactly 64 times. `tile_counts`: the first tile of each scene has 128 live slots.
All inputs are finite; a program needn't handle non-finite values.
Results may differ from the reference program's by a relative error of at most 0.014.
Values may be sent and summed in bfloat16 or wider, within the bound.
A program may use at most 256 MiB of HBM per device.

```python
import jax
import jax.numpy as jnp
from jax import lax

D = 1024
GPT = 64
PARAMS = 8
K = 128
SIDE = 16
VIEWS = 2
TOK_DEV = 32
TILE_DEV = 4
SCENES = 2
TOKENS = 512
GAUSS = 32768
TILES = 64
OUTW = 512
CAP = 64


def draw_tile_counts(key, part):
    first, second = jax.random.split(jax.random.fold_in(key, 17))
    raw = jax.random.randint(first, (SCENES, TILES), 1, K + 1)
    heavy = jax.random.randint(second, (SCENES, TILES // TILE_DEV, 1), 0, 2)
    light = (raw + 3) // 4
    counts = jnp.where(heavy == 1, raw.reshape(SCENES, TILES // TILE_DEV, TILE_DEV), light.reshape(SCENES, TILES // TILE_DEV, TILE_DEV))
    counts = counts.reshape(SCENES, TILES)
    return counts.at[:, 0].set(K).astype(jnp.int32)


def draw_tile_lists(key, part):
    first, second, third = jax.random.split(jax.random.fold_in(key, 29), 3)
    owners = TILES // TILE_DEV
    slot_total = TILE_DEV * K
    blocks = SCENES * owners
    own_count = TOK_DEV * GPT
    busiest = jax.random.randint(first, (blocks, 1), 0, owners)
    place = jnp.arange(slot_total, dtype=jnp.int32)[None, :]
    others = (busiest + 1 + (place - CAP) % (owners - 1)) % owners
    owner = jnp.where(place < CAP, busiest, others)
    scores = jax.random.randint(second, (blocks, slot_total), 0, slot_total) * slot_total + place
    order = jnp.argsort(scores, axis=1)
    owner = jnp.take_along_axis(owner, order, axis=1)
    within = jax.random.randint(third, (blocks, slot_total), 0, own_count)
    lists = owner * own_count + within
    return lists.reshape(SCENES, TILES, K).astype(jnp.int32)


def shard_levels(stream_key, extent, cuts, smallest, top_value):
    def one(position, parts):
        draws = jax.random.uniform(jax.random.fold_in(jax.random.fold_in(stream_key, 6), position), (parts,), jnp.float32, smallest / len(cuts), top_value / len(cuts))
        return jnp.repeat(jnp.exp(draws), extent[position] // parts).reshape((-1,) + (1,) * (len(extent) - position - 1))

    factor_of = one(*cuts[0])
    for cut in cuts[1:]:
        factor_of = factor_of * one(*cut)
    return factor_of


def scatter_about(rng, extent, width, limit, pieces=(), held_as=jnp.bfloat16):
    values = width * jax.random.normal(rng, extent, jnp.float32)
    if pieces:
        values = values * shard_levels(rng, extent, pieces, -0.22, 0.18)
    return jnp.clip(values, -limit, limit).astype(held_as)


def setup_inputs(seed: int = 0) -> dict:
    seeds = jax.random.split(jax.random.key(seed), 8)
    return {
        "tokens": scatter_about(seeds[0], (SCENES, TOKENS, D), 1.0, 6.0, ((0, 2), (1, 16))),
        "norm_gain": jnp.clip(1.0 + 0.18 * jax.random.normal(seeds[1], (D,), jnp.float32), 0.1, 1.9),
        "head_weight": scatter_about(seeds[2], (D, OUTW), D ** -0.5, 0.1875),
        "tile_lists": draw_tile_lists(jax.random.fold_in(seeds[7], 71), 0),
        "tile_counts": draw_tile_counts(jax.random.fold_in(seeds[7], 71), 0),
        "cameras": scatter_about(seeds[5], (SCENES, VIEWS, 8), 0.8, 3.0, ((0, 2),), jnp.float32),
        "targets": jnp.clip(1.0 * jax.random.uniform(seeds[6], (SCENES, TILES, 3 * SIDE * SIDE), jnp.float32) ** shard_levels(seeds[6], (SCENES, TILES, 3 * SIDE * SIDE), ((0, 2), (1, 16)), -0.2, 0.2), 0.0, 1.0).astype(jnp.bfloat16),
    }


def pixel_grid():
    place = jnp.arange(SIDE * SIDE, dtype=jnp.int32)
    across = ((place % SIDE).astype(jnp.float32) + 0.5) * (2.0 / SIDE) - 1.0
    down = ((place // SIDE).astype(jnp.float32) + 0.5) * (2.0 / SIDE) - 1.0
    return (across, down)

def composite(values, live, cams, wanted, across, down):
    slots = jnp.arange(K, dtype=jnp.int32)
    strict = (slots[:, None] < slots[None, :]).astype(jnp.float32)
    sx = jnp.tanh(cams[:, 0:1] * values[0] + cams[:, 1:2] * values[1] + cams[:, 2:3] * values[2] + cams[:, 3:4])
    sy = jnp.tanh(cams[:, 4:5] * values[0] + cams[:, 5:6] * values[1] + cams[:, 6:7] * values[2] + cams[:, 7:8])
    spread = jnp.exp(-2.0 * values[3])
    dxx = across[None, None, :] - sx[:, :, None]
    dyy = down[None, None, :] - sy[:, :, None]
    alpha = 0.3 * jax.nn.sigmoid(values[4])[:, :, None] * jnp.exp(-0.5 * (dxx * dxx + dyy * dyy) * spread[:, :, None]) * live[:, :, None]
    logs = jnp.log1p(-alpha)
    before = jnp.einsum('bkp,kj->bjp', logs, strict, precision=lax.Precision.HIGHEST)
    weight = alpha * jnp.exp(before)
    colour = jnp.einsum('bkp,cbk->bcp', weight, jax.nn.sigmoid(values[5:8]), precision=lax.Precision.HIGHEST)
    colour = colour.reshape(colour.shape[0], 3 * SIDE * SIDE)
    diff = colour - wanted.astype(jnp.float32)
    return (jnp.sum(diff * diff), colour)

def normalize(tokens_scene, norm_gain):
    values = tokens_scene.astype(jnp.float32)
    scale = lax.rsqrt(lax.optimization_barrier(jnp.mean(values * values, axis=-1, keepdims=True)) + 1e-06)
    return (values * scale * norm_gain).astype(jnp.bfloat16)

def scene_pass(tokens_scene, norm_gain, head_weight, lists, counts, cams, wanted, factor):
    normed = normalize(tokens_scene, norm_gain)
    head = jnp.dot(normed, head_weight, preferred_element_type=jnp.float32)
    gauss = head.reshape(TOKENS, PARAMS, GPT).transpose(1, 0, 2).reshape(PARAMS, GAUSS).astype(jnp.bfloat16)
    gauss_f = gauss.astype(jnp.float32)
    per_view = TILES // VIEWS
    which = jnp.arange(TILES, dtype=jnp.int32) // per_view
    onehot = (which[:, None] == jnp.arange(VIEWS, dtype=jnp.int32)[None, :]).astype(jnp.float32)
    tile_cams = jnp.dot(onehot, cams, precision=lax.Precision.HIGHEST)
    blocks = TILES // TILE_DEV
    across, down = pixel_grid()
    slots = jnp.arange(K, dtype=jnp.int32)

    def step(carry, inputs):
        dense, total = carry
        lb, cb, camb, wb = inputs
        values = jnp.take(gauss_f, lb.astype(jnp.int32), axis=1)
        live = (slots[None, :] < cb[:, None]).astype(jnp.float32)

        def local(vals):
            return composite(vals, live, camb, wb, across, down)
        part, pullback, colour = jax.vjp(local, values, has_aux=True)
        grads = pullback(jnp.ones_like(part) * factor)[0]
        dense = dense.at[:, lb.reshape(-1)].add(grads.reshape(PARAMS, -1))
        return ((dense, total + part * factor), colour.astype(jnp.bfloat16))
    start = (jnp.zeros((PARAMS, GAUSS), jnp.float32), jnp.zeros((), jnp.float32))
    inputs = (lists.reshape(blocks, TILE_DEV, K), counts.reshape(blocks, TILE_DEV), tile_cams.reshape(blocks, TILE_DEV, 8), wanted.reshape(blocks, TILE_DEV, 3 * SIDE * SIDE))
    (dense, total), images = lax.scan(step, start, inputs)
    dhead = dense.reshape(PARAMS, TOKENS, GPT).transpose(1, 0, 2).reshape(TOKENS, PARAMS * GPT)
    grad = jnp.dot(normed.astype(jnp.float32).T, dhead, precision=lax.Precision.HIGHEST)
    return (images.reshape(TILES, 3 * SIDE * SIDE), grad, total)

def reference(tokens, norm_gain, head_weight, tile_lists, tile_counts, cameras, targets):
    factor = 1.0 / (SCENES * TILES)
    images = []
    grad_head = jnp.zeros((D, PARAMS * GPT), jnp.float32)
    loss = jnp.zeros((), jnp.float32)
    for scene in range(SCENES):
        image_s, grad_s, loss_s = scene_pass(tokens[scene], norm_gain, head_weight, tile_lists[scene], tile_counts[scene], cameras[scene], targets[scene], factor)
        images.append(image_s)
        grad_head = grad_head + grad_s
        loss = loss + loss_s
    return (jnp.stack(images), grad_head, loss)
```

```python
import functools

import jax
import jax.numpy as jnp
from jax import lax
from jax.experimental import pallas as pl
from jax.experimental.pallas import tpu as pltpu
from jax.sharding import PartitionSpec as P

PARAMS = 8
SIDE = 16
VIEWS = 2
MESH = pl.DeviceIdType.MESH
F32 = jnp.float32
BF16 = jnp.bfloat16
NN = (((1,), (0,)), ((), ()))
NT = (((1,), (1,)), ((), ()))
TN = (((0,), (0,)), ((), ()))


def mm(a, b, dims):
    return lax.dot_general(a, b, dims, preferred_element_type=F32)


def split(x):
    hi = x.astype(BF16)
    lo = (x - hi.astype(F32)).astype(BF16)
    return hi, lo


def mm2(a, x, dims):
    hi, lo = split(x)
    return mm(a, hi, dims) + mm(a, lo, dims)


def mm3(x, y, dims):
    xh, xl = split(x)
    yh, yl = split(y)
    return mm(xh, yh, dims) + mm(xh, yl, dims) + mm(xl, yh, dims)


def sigmoid(x):
    return 1.0 / (1.0 + jnp.exp(-x))


def pick(row, tokens, gpt):
    tok = row // gpt
    at = lax.broadcasted_iota(jnp.int32, (tokens, row.shape[1]), 0)
    return jnp.where(at == tok, 1.0, 0.0).astype(BF16)


def kernel(
    nsec, nview, factor,
    tok_ref, gain_ref, w_ref, list_ref, count_ref, cam_ref, want_ref,
    image_ref, grad_ref, loss_ref,
    heads, norms, lists, grads, dhead, mine, theirs, loss_mine, loss_theirs,
    s_list, r_list, s_head, r_head, s_norm, r_norm, s_grad, r_grad, s_part, r_part, s_loss, r_loss,
):
    group = nsec * nview
    sec, view, scene = lax.axis_index("section"), lax.axis_index("view"), lax.axis_index("scene")
    me = sec * nview + view
    tok_rows, width = tok_ref.shape
    outw = w_ref.shape[1]
    gpt = outw // PARAMS
    tiles, K = list_ref.shape
    tokens = group * tok_rows
    pix = SIDE * SIDE

    def peer(i):
        j = lax.rem(me + i, group)
        return j, (j // nview, lax.rem(j, nview), scene)

    partner = (sec, view, 1 - scene)

    barrier = pltpu.get_barrier_semaphore()

    @pl.loop(1, group)
    def _(i):
        pl.semaphore_signal(barrier, inc=1, device_id=peer(i)[1], device_id_type=MESH)

    pl.semaphore_signal(barrier, inc=1, device_id=partner, device_id_type=MESH)

    x = tok_ref[...].astype(F32)
    scale = lax.rsqrt(jnp.mean(x * x, axis=-1, keepdims=True) + 1e-06)
    normed = (x * scale * gain_ref[...]).astype(BF16)
    norms[me] = normed
    heads[me] = mm(normed, w_ref[...], NN).astype(BF16)
    lists[me] = list_ref[...]

    pl.semaphore_wait(barrier, group)

    def push(buf, src, send, recv, i):
        j, where = peer(i)
        return pltpu.make_async_remote_copy(
            src_ref=src, dst_ref=buf.at[me], send_sem=send.at[i], recv_sem=recv.at[me],
            device_id=where, device_id_type=MESH,
        )

    def take(buf, send, recv, j):
        pltpu.make_async_remote_copy(
            src_ref=buf.at[j], dst_ref=buf.at[j], send_sem=send.at[0], recv_sem=recv.at[j],
            device_id=partner, device_id_type=MESH,
        ).wait_recv()

    def take_all(buf, send, recv):
        @pl.loop(1, group)
        def _(i):
            take(buf, send, recv, peer(i)[0])

    @pl.loop(1, group)
    def _(i):
        push(heads, heads.at[me], s_head, r_head, i).start()

    @pl.loop(1, group)
    def _(i):
        push(lists, list_ref, s_list, r_list, i).start()

    @pl.loop(1, group)
    def _(i):
        push(norms, norms.at[me], s_norm, r_norm, i).start()

    own = jnp.concatenate([list_ref[pl.ds(b, 1), :] for b in range(tiles)], axis=1)
    hot = pick(own, tokens, gpt)
    inner = own - (own // gpt) * gpt
    at_g = lax.broadcasted_iota(jnp.int32, (gpt, tiles * K), 0)
    mask = jnp.where(at_g == inner, 1.0, 0.0)

    take_all(heads, s_head, r_head)
    table = heads[...].reshape(tokens, outw)
    picked = mm(table, hot, TN)
    rows = [
        jnp.sum(picked[p * gpt : (p + 1) * gpt] * mask, axis=0, keepdims=True)
        for p in range(PARAMS)
    ]

    place = lax.broadcasted_iota(jnp.int32, (1, pix), 1)
    across = ((place % SIDE).astype(F32) + 0.5) * (2.0 / SIDE) - 1.0
    down = ((place // SIDE).astype(F32) + 0.5) * (2.0 / SIDE) - 1.0
    ka = lax.broadcasted_iota(jnp.int32, (K, K), 0)
    kb = lax.broadcasted_iota(jnp.int32, (K, K), 1)
    lower = jnp.where(kb < ka, 1.0, 0.0).astype(BF16)
    upper = jnp.where(kb > ka, 1.0, 0.0).astype(BF16)
    ones = jnp.ones((8, pix), BF16)
    per_view = (tiles * group) // VIEWS
    slot = lax.broadcasted_iota(jnp.int32, (1, K), 1)
    zero_row = jnp.zeros((1, K), F32)

    for b in range(tiles):
        cut = slice(b * K, (b + 1) * K)
        mx, my, mz, ls, op, cr, cg, cb = [r[:, cut] for r in rows]
        vi = (me * tiles + b) // per_view
        cam = [cam_ref[vi, n] for n in range(8)]
        live = jnp.where(slot < count_ref[b], 1.0, 0.0)
        sx = jnp.tanh(cam[0] * mx + cam[1] * my + cam[2] * mz + cam[3])
        sy = jnp.tanh(cam[4] * mx + cam[5] * my + cam[6] * mz + cam[7])
        spread = jnp.exp(-2.0 * ls)
        sop = sigmoid(op)
        amp = 0.3 * sop * live
        shade = sigmoid(jnp.concatenate([cr, cg, cb], axis=0))
        shade8 = jnp.concatenate([shade, jnp.zeros((5, K), F32)], axis=0)
        cols = jnp.concatenate([sx, sy, spread, amp, jnp.zeros((K - 4, K), F32)], axis=0).T
        csx, csy, csp, camp = [cols[:, n : n + 1] for n in range(4)]
        dx = across - csx
        dy = down - csy
        r2 = dx * dx + dy * dy
        alpha = camp * jnp.exp(-0.5 * r2 * csp)
        rest = 1.0 - alpha
        trans = jnp.exp(mm2(lower, jnp.log(rest), NN))
        weight = alpha * trans
        colour = mm3(shade8, weight, NN)
        for c in range(3):
            image_ref[pl.ds(b, 1), c * pix : (c + 1) * pix] = colour[c : c + 1].astype(BF16)
        want = jnp.concatenate(
            [want_ref[pl.ds(b, 1), c * pix : (c + 1) * pix].astype(F32) for c in range(3)]
            + [jnp.zeros((5, pix), F32)],
            axis=0,
        )
        diff = colour - want
        sq = jnp.sum(diff * diff, axis=0, keepdims=True)
        part = sq[:, :K]
        for n in range(1, pix // K):
            part = part + sq[:, n * K : (n + 1) * K]
        part = part * factor
        dcol = (2.0 * factor) * diff
        dw = mm3(shade8, dcol, TN)
        dshade = mm3(dcol, weight, NT)
        dww = dw * weight
        dlogs = mm2(upper, dww, NN)
        h = dww - dlogs * alpha / rest
        s_h = mm2(ones, h, NT)[0:1]
        s_x = mm2(ones, h * dx, NT)[0:1]
        s_y = mm2(ones, h * dy, NT)[0:1]
        s_r = mm2(ones, h * r2, NT)[0:1]
        px = spread * s_x * (1.0 - sx * sx)
        py = spread * s_y * (1.0 - sy * sy)
        dcolour = dshade[0:3] * shade * (1.0 - shade)
        l0 = part.astype(BF16).astype(F32)
        l1 = (part - l0).astype(BF16).astype(F32)
        l2 = part - l0 - l1
        out = jnp.concatenate(
            [
                cam[0] * px + cam[4] * py,
                cam[1] * px + cam[5] * py,
                cam[2] * px + cam[6] * py,
                spread * s_r,
                (1.0 - sop) * s_h,
                dcolour,
                l0,
                l1,
                l2,
                jnp.zeros((5, K), F32),
            ],
            axis=0,
        )
        grads[me, :, cut] = out.astype(BF16)

    @pl.loop(1, group)
    def _(i):
        push(grads, grads.at[me], s_grad, r_grad, i).start()

    take_all(lists, s_list, r_list)
    dhead[...] = jnp.zeros_like(dhead)
    loss_mine[...] = jnp.zeros_like(loss_mine)

    @pl.loop(0, group)
    def _(j):
        row = jnp.concatenate([lists[j, pl.ds(b, 1), :] for b in range(tiles)], axis=1)
        where = pick(row, tokens, gpt)
        g = row - (row // gpt) * gpt
        fits = lax.broadcasted_iota(jnp.int32, (gpt, tiles * K), 0) == g

        @pl.when(j != me)
        def _():
            take(grads, s_grad, r_grad, j)

        got = grads[j].astype(F32)
        spreadout = jnp.concatenate(
            [jnp.where(fits, got[p : p + 1], 0.0).astype(BF16) for p in range(PARAMS)], axis=0
        )
        dhead[...] += mm(where, spreadout, NT)
        lossy = got[8:9] + got[9:10] + got[10:11]
        for b in range(tiles):
            loss_mine[0:1, :] += lossy[:, b * K : (b + 1) * K]

    take_all(norms, s_norm, r_norm)
    loss_copy = pltpu.make_async_remote_copy(
        src_ref=loss_mine, dst_ref=loss_theirs, send_sem=s_loss, recv_sem=r_loss,
        device_id=partner, device_id_type=MESH,
    )
    dh = dhead[...].astype(BF16)
    dhead_rows = 256
    chunks = width // dhead_rows

    def part_copy(n):
        span = pl.ds(n * dhead_rows, dhead_rows)
        return pltpu.make_async_remote_copy(
            src_ref=mine.at[span], dst_ref=theirs.at[span],
            send_sem=s_part.at[n], recv_sem=r_part.at[n],
            device_id=partner, device_id_type=MESH,
        )

    for n in range(chunks):
        a = norms[:, :, n * dhead_rows : (n + 1) * dhead_rows].reshape(tokens, dhead_rows)
        mine[n * dhead_rows : (n + 1) * dhead_rows, :] = mm(a, dh, TN).astype(BF16)
        if n == 0:
            loss_copy.start()
        else:
            part_copy(n - 1).start()
    part_copy(chunks - 1).start()

    for n in range(chunks):
        part_copy(n).wait_recv()
        span = slice(n * dhead_rows, (n + 1) * dhead_rows)
        grad_ref[span, :] = mine[span, :].astype(F32) + theirs[span, :].astype(F32)
    loss_copy.wait_recv()
    loss_ref[...] = jnp.broadcast_to(
        jnp.sum(loss_mine[...] + loss_theirs[...], keepdims=True), loss_ref.shape
    )

    loss_copy.wait_send()
    for n in range(chunks):
        part_copy(n).wait_send()

    @pl.loop(1, group)
    def _(i):
        push(heads, heads.at[me], s_head, r_head, i).wait_send()
        push(lists, list_ref, s_list, r_list, i).wait_send()
        push(norms, norms.at[me], s_norm, r_norm, i).wait_send()
        push(grads, grads.at[me], s_grad, r_grad, i).wait_send()


def solution(mesh):
    nsec, nview, nscene = mesh.shape["section"], mesh.shape["view"], mesh.shape["scene"]
    group = nsec * nview

    def body(tokens, norm_gain, head_weight, tile_lists, tile_counts, cameras, targets):
        tok_rows, width = tokens.shape[1:]
        outw = head_weight.shape[1]
        tiles, K = tile_lists.shape[1:]
        factor = 1.0 / (nscene * tiles * group)
        vmem = pl.BlockSpec(memory_space=pltpu.VMEM)
        smem = pl.BlockSpec(memory_space=pltpu.SMEM)
        dma = pltpu.SemaphoreType.DMA
        image, grad, loss = pl.pallas_call(
            functools.partial(kernel, nsec, nview, factor),
            out_shape=(
                jax.ShapeDtypeStruct((tiles, targets.shape[2]), BF16),
                jax.ShapeDtypeStruct((width, outw), F32),
                jax.ShapeDtypeStruct((8, 128), F32),
            ),
            in_specs=[vmem, vmem, vmem, vmem, smem, smem, vmem],
            out_specs=(vmem, vmem, vmem),
            scratch_shapes=[
                pltpu.VMEM((group, tok_rows, outw), BF16),
                pltpu.VMEM((group, tok_rows, width), BF16),
                pltpu.VMEM((group, tiles, K), jnp.int32),
                pltpu.VMEM((group, 16, tiles * K), BF16),
                pltpu.VMEM((group * tok_rows, outw), F32),
                pltpu.VMEM((width, outw), BF16),
                pltpu.VMEM((width, outw), BF16),
                pltpu.VMEM((8, K), F32),
                pltpu.VMEM((8, K), F32),
            ]
            + [dma((group,))] * 8
            + [dma((width // 256,))] * 2
            + [dma, dma],
            compiler_params=pltpu.CompilerParams(
                collective_id=0, has_side_effects=True, vmem_limit_bytes=60 * 1024 * 1024
            ),
        )(
            tokens[0], norm_gain[None], head_weight, tile_lists[0], tile_counts[0], cameras[0],
            targets[0],
        )
        return image[None], grad, loss[0, 0]

    in_specs = (
        P("scene", ("section", "view"), None),
        P(),
        P(),
        P("scene", ("section", "view"), None),
        P("scene", ("section", "view")),
        P("scene", None, None),
        P("scene", ("section", "view"), None),
    )
    out_specs = (P("scene", ("section", "view"), None), P(), P())
    return jax.shard_map(body, mesh=mesh, in_specs=in_specs, out_specs=out_specs, check_vma=False)
```

```python
import functools

import jax
import jax.numpy as jnp
from jax import lax
from jax.experimental import pallas as pl
from jax.experimental.pallas import tpu as pltpu
from jax.sharding import PartitionSpec as P

PARAMS = 8
SIDE = 16
VIEWS = 2
MESH = pl.DeviceIdType.MESH
F32 = jnp.float32
BF16 = jnp.bfloat16
NN = (((1,), (0,)), ((), ()))
NT = (((1,), (1,)), ((), ()))
TN = (((0,), (0,)), ((), ()))


def mm(a, b, dims):
    return lax.dot_general(a, b, dims, preferred_element_type=F32)


def split(x):
    hi = x.astype(BF16)
    lo = (x - hi.astype(F32)).astype(BF16)
    return hi, lo


def mm2(a, x, dims):
    hi, lo = split(x)
    return mm(a, hi, dims) + mm(a, lo, dims)


def mm3(x, y, dims):
    xh, xl = split(x)
    yh, yl = split(y)
    return mm(xh, yh, dims) + mm(xh, yl, dims) + mm(xl, yh, dims)


def sigmoid(x):
    return 1.0 / (1.0 + jnp.exp(-x))


def pick(row, tokens, gpt):
    tok = row // gpt
    at = lax.broadcasted_iota(jnp.int32, (tokens, row.shape[1]), 0)
    return jnp.where(at == tok, 1.0, 0.0).astype(BF16)


def kernel(
    nsec, nview, factor,
    tok_ref, gain_ref, w_ref, list_ref, count_ref, cam_ref, want_ref,
    image_ref, grad_ref, loss_ref,
    heads, norms, lists, grads, dhead, mine, theirs, loss_mine, loss_theirs,
    s_list, r_list, s_head, r_head, s_norm, r_norm, s_grad, r_grad, s_part, r_part, s_loss, r_loss,
):
    group = nsec * nview
    sec, view, scene = lax.axis_index("section"), lax.axis_index("view"), lax.axis_index("scene")
    me = sec * nview + view
    tok_rows, width = tok_ref.shape
    outw = w_ref.shape[1]
    gpt = outw // PARAMS
    tiles, K = list_ref.shape
    tokens = group * tok_rows
    pix = SIDE * SIDE

    def peer(i):
        j = lax.rem(me + i, group)
        return j, (j // nview, lax.rem(j, nview), scene)

    def along_view(i):
        v = lax.rem(view + i, nview)
        return sec * nview + v, (sec, v, scene)

    def along_section(i):
        s = lax.rem(sec + i, nsec)
        return s, (s, view, scene)

    partner = (sec, view, 1 - scene)

    barrier = pltpu.get_barrier_semaphore()

    @pl.loop(1, group)
    def _(i):
        pl.semaphore_signal(barrier, inc=1, device_id=peer(i)[1], device_id_type=MESH)

    pl.semaphore_signal(barrier, inc=1, device_id=partner, device_id_type=MESH)

    x = tok_ref[...].astype(F32)
    scale = lax.rsqrt(jnp.mean(x * x, axis=-1, keepdims=True) + 1e-06)
    normed = (x * scale * gain_ref[...]).astype(BF16)
    norms[me] = normed
    heads[me] = mm(normed, w_ref[...], NN).astype(BF16)
    lists[me] = list_ref[...]

    pl.semaphore_wait(barrier, group)

    def push(buf, src, send, recv, i):
        j, where = peer(i)
        return pltpu.make_async_remote_copy(
            src_ref=src, dst_ref=buf.at[me], send_sem=send.at[i], recv_sem=recv.at[me],
            device_id=where, device_id_type=MESH,
        )

    def take(buf, send, recv, j):
        pltpu.make_async_remote_copy(
            src_ref=buf.at[j], dst_ref=buf.at[j], send_sem=send.at[0], recv_sem=recv.at[j],
            device_id=partner, device_id_type=MESH,
        ).wait_recv()

    def take_all(buf, send, recv):
        @pl.loop(1, group)
        def _(i):
            take(buf, send, recv, peer(i)[0])

    def first(buf, send, recv, i):
        return pltpu.make_async_remote_copy(
            src_ref=buf.at[me], dst_ref=buf.at[me], send_sem=send.at[i], recv_sem=recv.at[me],
            device_id=along_view(i)[1], device_id_type=MESH,
        )

    def relay(buf, send, recv, i, k):
        j = along_view(i)[0]
        return pltpu.make_async_remote_copy(
            src_ref=buf.at[j], dst_ref=buf.at[j],
            send_sem=send.at[nview + i * (nsec - 1) + k - 1], recv_sem=recv.at[j],
            device_id=along_section(k)[1], device_id_type=MESH,
        )

    def spread_own(buf, send, recv):
        for k in range(1, nsec):
            relay(buf, send, recv, 0, k).start()

        @pl.loop(1, nview)
        def _(i):
            first(buf, send, recv, i).start()

    def spread_rest(buf, send, recv):
        @pl.loop(1, nview)
        def _(i):
            take(buf, send, recv, along_view(i)[0])
            for k in range(1, nsec):
                relay(buf, send, recv, i, k).start()

    def collect(buf, send, recv):
        for k in range(1, nsec):
            s = along_section(k)[0]

            @pl.loop(0, nview)
            def _(i):
                take(buf, send, recv, s * nview + lax.rem(view + i, nview))

    def drain(buf, send, recv):
        @pl.loop(1, nview)
        def _(i):
            first(buf, send, recv, i).wait_send()

        @pl.loop(0, nview)
        def _(i):
            for k in range(1, nsec):
                relay(buf, send, recv, i, k).wait_send()

    @pl.loop(1, group)
    def _(i):
        push(lists, list_ref, s_list, r_list, i).start()

    spread_own(heads, s_head, r_head)

    own = jnp.concatenate([list_ref[pl.ds(b, 1), :] for b in range(tiles)], axis=1)
    hot = pick(own, tokens, gpt)
    inner = own - (own // gpt) * gpt
    at_g = lax.broadcasted_iota(jnp.int32, (gpt, tiles * K), 0)
    mask = jnp.where(at_g == inner, 1.0, 0.0)

    spread_rest(heads, s_head, r_head)
    collect(heads, s_head, r_head)
    spread_own(norms, s_norm, r_norm)
    table = heads[...].reshape(tokens, outw)
    picked = mm(table, hot, TN)
    rows = [
        jnp.sum(picked[p * gpt : (p + 1) * gpt] * mask, axis=0, keepdims=True)
        for p in range(PARAMS)
    ]

    place = lax.broadcasted_iota(jnp.int32, (1, pix), 1)
    across = ((place % SIDE).astype(F32) + 0.5) * (2.0 / SIDE) - 1.0
    down = ((place // SIDE).astype(F32) + 0.5) * (2.0 / SIDE) - 1.0
    ka = lax.broadcasted_iota(jnp.int32, (K, K), 0)
    kb = lax.broadcasted_iota(jnp.int32, (K, K), 1)
    lower = jnp.where(kb < ka, 1.0, 0.0).astype(BF16)
    upper = jnp.where(kb > ka, 1.0, 0.0).astype(BF16)
    ones = jnp.ones((8, pix), BF16)
    per_view = (tiles * group) // VIEWS
    slot = lax.broadcasted_iota(jnp.int32, (1, K), 1)
    zero_row = jnp.zeros((1, K), F32)

    for b in range(tiles):
        cut = slice(b * K, (b + 1) * K)
        mx, my, mz, ls, op, cr, cg, cb = [r[:, cut] for r in rows]
        vi = (me * tiles + b) // per_view
        cam = [cam_ref[vi, n] for n in range(8)]
        live = jnp.where(slot < count_ref[b], 1.0, 0.0)
        sx = jnp.tanh(cam[0] * mx + cam[1] * my + cam[2] * mz + cam[3])
        sy = jnp.tanh(cam[4] * mx + cam[5] * my + cam[6] * mz + cam[7])
        spread = jnp.exp(-2.0 * ls)
        sop = sigmoid(op)
        amp = 0.3 * sop * live
        shade = sigmoid(jnp.concatenate([cr, cg, cb], axis=0))
        shade8 = jnp.concatenate([shade, jnp.zeros((5, K), F32)], axis=0)
        cols = jnp.concatenate([sx, sy, spread, amp, jnp.zeros((K - 4, K), F32)], axis=0).T
        csx, csy, csp, camp = [cols[:, n : n + 1] for n in range(4)]
        dx = across - csx
        dy = down - csy
        r2 = dx * dx + dy * dy
        alpha = camp * jnp.exp(-0.5 * r2 * csp)
        rest = 1.0 - alpha
        trans = jnp.exp(mm2(lower, jnp.log(rest), NN))
        weight = alpha * trans
        colour = mm3(shade8, weight, NN)
        for c in range(3):
            image_ref[pl.ds(b, 1), c * pix : (c + 1) * pix] = colour[c : c + 1].astype(BF16)
        want = jnp.concatenate(
            [want_ref[pl.ds(b, 1), c * pix : (c + 1) * pix].astype(F32) for c in range(3)]
            + [jnp.zeros((5, pix), F32)],
            axis=0,
        )
        diff = colour - want
        sq = jnp.sum(diff * diff, axis=0, keepdims=True)
        part = sq[:, :K]
        for n in range(1, pix // K):
            part = part + sq[:, n * K : (n + 1) * K]
        part = part * factor
        dcol = (2.0 * factor) * diff
        dw = mm3(shade8, dcol, TN)
        dshade = mm3(dcol, weight, NT)
        dww = dw * weight
        dlogs = mm2(upper, dww, NN)
        h = dww - dlogs * alpha / rest
        s_h = mm2(ones, h, NT)[0:1]
        s_x = mm2(ones, h * dx, NT)[0:1]
        s_y = mm2(ones, h * dy, NT)[0:1]
        s_r = mm2(ones, h * r2, NT)[0:1]
        px = spread * s_x * (1.0 - sx * sx)
        py = spread * s_y * (1.0 - sy * sy)
        dcolour = dshade[0:3] * shade * (1.0 - shade)
        l0 = part.astype(BF16).astype(F32)
        l1 = (part - l0).astype(BF16).astype(F32)
        l2 = part - l0 - l1
        out = jnp.concatenate(
            [
                cam[0] * px + cam[4] * py,
                cam[1] * px + cam[5] * py,
                cam[2] * px + cam[6] * py,
                spread * s_r,
                (1.0 - sop) * s_h,
                dcolour,
                l0,
                l1,
                l2,
                jnp.zeros((5, K), F32),
            ],
            axis=0,
        )
        grads[me, :, cut] = out.astype(BF16)

    @pl.loop(1, group)
    def _(i):
        push(grads, grads.at[me], s_grad, r_grad, i).start()

    spread_rest(norms, s_norm, r_norm)
    take_all(lists, s_list, r_list)
    dhead[...] = jnp.zeros_like(dhead)
    loss_mine[...] = jnp.zeros_like(loss_mine)

    @pl.loop(0, group)
    def _(j):
        row = jnp.concatenate([lists[j, pl.ds(b, 1), :] for b in range(tiles)], axis=1)
        where = pick(row, tokens, gpt)
        g = row - (row // gpt) * gpt
        fits = lax.broadcasted_iota(jnp.int32, (gpt, tiles * K), 0) == g

        @pl.when(j != me)
        def _():
            take(grads, s_grad, r_grad, j)

        got = grads[j].astype(F32)
        spreadout = jnp.concatenate(
            [jnp.where(fits, got[p : p + 1], 0.0).astype(BF16) for p in range(PARAMS)], axis=0
        )
        dhead[...] += mm(where, spreadout, NT)
        lossy = got[8:9] + got[9:10] + got[10:11]
        for b in range(tiles):
            loss_mine[0:1, :] += lossy[:, b * K : (b + 1) * K]

    collect(norms, s_norm, r_norm)
    loss_copy = pltpu.make_async_remote_copy(
        src_ref=loss_mine, dst_ref=loss_theirs, send_sem=s_loss, recv_sem=r_loss,
        device_id=partner, device_id_type=MESH,
    )
    dh = dhead[...].astype(BF16)
    dhead_rows = 256
    chunks = width // dhead_rows

    def part_copy(n):
        span = pl.ds(n * dhead_rows, dhead_rows)
        return pltpu.make_async_remote_copy(
            src_ref=mine.at[span], dst_ref=theirs.at[span],
            send_sem=s_part.at[n], recv_sem=r_part.at[n],
            device_id=partner, device_id_type=MESH,
        )

    for n in range(chunks):
        a = norms[:, :, n * dhead_rows : (n + 1) * dhead_rows].reshape(tokens, dhead_rows)
        mine[n * dhead_rows : (n + 1) * dhead_rows, :] = mm(a, dh, TN).astype(BF16)
        if n == 0:
            loss_copy.start()
        else:
            part_copy(n - 1).start()
    part_copy(chunks - 1).start()

    for n in range(chunks):
        part_copy(n).wait_recv()
        span = slice(n * dhead_rows, (n + 1) * dhead_rows)
        grad_ref[span, :] = (mine[span, :].astype(F32) + theirs[span, :].astype(F32)).astype(BF16)
    loss_copy.wait_recv()
    loss_ref[...] = jnp.broadcast_to(
        jnp.sum(loss_mine[...] + loss_theirs[...], keepdims=True), loss_ref.shape
    )

    loss_copy.wait_send()
    for n in range(chunks):
        part_copy(n).wait_send()

    @pl.loop(1, group)
    def _(i):
        push(lists, list_ref, s_list, r_list, i).wait_send()
        push(grads, grads.at[me], s_grad, r_grad, i).wait_send()

    drain(heads, s_head, r_head)
    drain(norms, s_norm, r_norm)


def solution(mesh):
    nsec, nview, nscene = mesh.shape["section"], mesh.shape["view"], mesh.shape["scene"]
    group = nsec * nview

    def body(tokens, norm_gain, head_weight, tile_lists, tile_counts, cameras, targets):
        tok_rows, width = tokens.shape[1:]
        outw = head_weight.shape[1]
        tiles, K = tile_lists.shape[1:]
        factor = 1.0 / (nscene * tiles * group)
        vmem = pl.BlockSpec(memory_space=pltpu.VMEM)
        smem = pl.BlockSpec(memory_space=pltpu.SMEM)
        dma = pltpu.SemaphoreType.DMA
        image, grad, loss = pl.pallas_call(
            functools.partial(kernel, nsec, nview, factor),
            out_shape=(
                jax.ShapeDtypeStruct((tiles, targets.shape[2]), BF16),
                jax.ShapeDtypeStruct((width, outw), BF16),
                jax.ShapeDtypeStruct((8, 128), F32),
            ),
            in_specs=[vmem, vmem, vmem, vmem, smem, smem, vmem],
            out_specs=(vmem, vmem, vmem),
            scratch_shapes=[
                pltpu.VMEM((group, tok_rows, outw), BF16),
                pltpu.VMEM((group, tok_rows, width), BF16),
                pltpu.VMEM((group, tiles, K), jnp.int32),
                pltpu.VMEM((group, 16, tiles * K), BF16),
                pltpu.VMEM((group * tok_rows, outw), F32),
                pltpu.VMEM((width, outw), BF16),
                pltpu.VMEM((width, outw), BF16),
                pltpu.VMEM((8, K), F32),
                pltpu.VMEM((8, K), F32),
            ]
            + [dma((group,))] * 2
            + [dma((nview * nsec,)), dma((group,))] * 2
            + [dma((group,))] * 2
            + [dma((width // 256,))] * 2
            + [dma, dma],
            compiler_params=pltpu.CompilerParams(
                collective_id=0, has_side_effects=True, vmem_limit_bytes=60 * 1024 * 1024
            ),
        )(
            tokens[0], norm_gain[None], head_weight, tile_lists[0], tile_counts[0], cameras[0],
            targets[0],
        )
        return image[None], grad.astype(F32), loss[0, 0]

    in_specs = (
        P("scene", ("section", "view"), None),
        P(),
        P(),
        P("scene", ("section", "view"), None),
        P("scene", ("section", "view")),
        P("scene", None, None),
        P("scene", ("section", "view"), None),
    )
    out_specs = (P("scene", ("section", "view"), None), P(), P())
    return jax.shard_map(body, mesh=mesh, in_specs=in_specs, out_specs=out_specs, check_vma=False)
```
